32 devices in a mesh: ctx: 8 (over z, x), head: 4 (over y, core).
Axes of the slice: x: 2, y: 2, z: 4, core: 2. Of those that a mesh axis runs over, the one named last changes fastest.
Arguments:
- queries: bfloat16 [16384, 128], P(('ctx', 'head')), may hold values from -6 to 6
- keys: bfloat16 [16384, 128], P(('ctx', 'head')), may hold values from -0.0625 to 0.0625
- values: bfloat16 [16384, 4096], P('ctx', 'head'), may hold values from -6 to 6
- tier_weight_rows: int32 [8, 16384], P(None, 'ctx'), may hold values from 0 to 15
- level_table: float32 [16, 32], P(None, 'head'), may hold values from 0.1 to 10
Outputs:
- mixed: bfloat16 [16384, 4096], P('ctx', 'head')
The draws below stay inside these ranges and needn't reach their ends.
All inputs are finite; a program needn't handle non-finite values.
Results may differ from the reference program's by a relative error of at most 0.0049.
Values may be sent and summed in bfloat16 or wider, within the bound.
No kernel may reach another device: no remote copies, remote signals or barrier semaphores. Data moves between devices by JAX's collectives and lax.ppermute only.
A program may use at most 192 MiB of HBM per device.

```python
import math
import jax
import jax.numpy as jnp
from jax import lax

HEADS = 32
HEAD_DIM = 128
KEY_DIM = 128
GROUP = 128
CLASSES = 16
TOKENS = 16384
TIER_COUNT = 8


def set_ends(array, key, low, high):
    longest = array.shape.index(max(array.shape))
    spots = []
    for shift in (0, 1):
        where = [jax.random.randint(jax.random.fold_in(key, axis), (), 0, length) for axis, length in enumerate(array.shape)]
        where[longest] = (where[longest] + shift) % array.shape[longest]
        spots.append(tuple(where))
    return array.at[spots[0]].set(low).at[spots[1]].set(high)


def shard_levels(stream_key, dims, shards, smallest, high):
    factor_of = 1.0
    for dim, shards_of in shards:
        steps = jax.random.uniform(jax.random.fold_in(jax.random.fold_in(stream_key, 6), dim), (shards_of,), jnp.float32, smallest / len(shards), high / len(shards))
        factor_of = factor_of * jnp.repeat(jnp.exp(steps), dims[dim] // shards_of).reshape((-1,) + (1,) * (len(dims) - 1 - dim))
    return factor_of


def noise(stream_key, extent, spread, most, shards=(), held_as=jnp.bfloat16):
    drawn = jax.random.normal(stream_key, extent, jnp.float32) * spread
    if len(shards) > 0:
        drawn = shard_levels(stream_key, extent, shards, -0.22, 0.18) * drawn
    return jnp.clip(drawn, min=-most, max=most).astype(held_as)


def setup_inputs(seed: int = 0) -> dict:
    splits = jax.random.split(jax.random.key(seed), 6)
    return {
        "queries": noise(splits[0], (TOKENS, KEY_DIM), 1.0, 6.0, ((0, 32),)),
        "keys": noise(splits[1], (TOKENS, KEY_DIM), (TOKENS // 2) ** -0.5, 0.0625, ((0, 32),)),
        "values": noise(splits[2], (TOKENS, HEADS * HEAD_DIM), 1.0, 6.0, ((0, 8), (1, 4))),
        "tier_weight_rows": set_ends(jax.random.randint(splits[3], (TIER_COUNT, TOKENS), 0, CLASSES), jax.random.fold_in(splits[3], 1), 0, CLASSES - 1).astype(jnp.int32),
        "level_table": jnp.clip(jnp.exp(math.log(10.0) - 4.6051702 * jax.random.uniform(splits[4], (CLASSES, HEADS), jnp.float32) ** shard_levels(splits[4], (CLASSES, HEADS), ((1, 4),), -0.2, 0.2)), 0.1, 10.0),
    }


def reference(queries, keys, values, tier_weight_rows, level_table):
    weights = level_table[tier_weight_rows]
    share = weights / jnp.sum(weights, axis=0)
    query_f = queries.astype(jnp.float32)
    key_f = keys.astype(jnp.float32)
    groups = TOKENS // GROUP
    scores = jnp.einsum("nik,njk->nij", query_f.reshape(groups, GROUP, KEY_DIM), key_f.reshape(groups, GROUP, KEY_DIM))
    causal = jnp.tril(jnp.ones((GROUP, GROUP), dtype=bool))
    scores = jnp.where(causal[None], scores, 0.0).astype(jnp.bfloat16)
    score_f = scores.astype(jnp.float32)
    per_head = values.reshape(TOKENS, HEADS, HEAD_DIM).transpose(1, 0, 2)
    shared_key_head = share.transpose(2, 0, 1)

    def one_head(pair):
        head_vals, lam = pair
        value_f = head_vals.astype(jnp.float32)
        near = jnp.einsum("nij,njd->nid", score_f, value_f.reshape(groups, GROUP, HEAD_DIM)).reshape(TOKENS, HEAD_DIM)
        total = lam[0][:, None] * near
        for level in range(1, TIER_COUNT):
            half = GROUP * 2 ** (level - 1)
            blocks = TOKENS // (2 * half)
            grouped_probe_matrix = key_f.reshape(blocks, 2, half, KEY_DIM)
            grouped_content_matrix = value_f.reshape(blocks, 2, half, HEAD_DIM)
            query_blocked = query_f.reshape(blocks, 2, half, KEY_DIM)
            cumulative_memory = jnp.einsum("rlx,rlh->rxh", grouped_probe_matrix[:, 0], grouped_content_matrix[:, 0])
            cumulative_memory = lax.optimization_barrier(cumulative_memory.astype(jnp.bfloat16)).astype(jnp.float32)
            upper_half_branch = jnp.einsum("hfp,hpo->hfo", query_blocked[:, 1], cumulative_memory)
            part = jnp.stack([jnp.zeros_like(upper_half_branch), upper_half_branch], axis=1).reshape(TOKENS, HEAD_DIM)
            total = total + lam[level][:, None] * part
        return total.astype(jnp.bfloat16)

    outs = lax.map(one_head, (per_head, shared_key_head))
    return outs.transpose(1, 0, 2).reshape(TOKENS, HEADS * HEAD_DIM)
```

```python
import functools

import jax
import jax.numpy as jnp
from jax import lax
from jax.experimental import pallas as pl
from jax.experimental.pallas import tpu as pltpu
from jax.sharding import PartitionSpec as P

GROUP = 128
F32 = jnp.float32
BF16 = jnp.bfloat16


def exchanged(value, axis, mask):
    pairs = [(source, source ^ mask) for source in range(lax.axis_size(axis))]
    return lax.ppermute(value, axis, pairs)


def dot(a, b):
    return jnp.dot(a, b, preferred_element_type=F32)


def place(pieces, me, target):
    rows = pieces[0].shape[0]
    for j, piece in enumerate(pieces):
        start = pl.multiple_of((me ^ j) * rows, rows)
        target[pl.ds(start, rows), :] = piece[...]


def state_kernel(count, place_ref, *refs):
    pieces, v_ref, s_ref, sb_ref, k_all, k_t = refs[:count], *refs[count:]

    @pl.when(pl.program_id(0) == 0)
    def _():
        place(pieces, place_ref[0], k_all)
        k_t[...] = k_all[...].T

    s = dot(k_t[...], v_ref[...])
    s_ref[...] = s
    sb_ref[...] = s.astype(BF16)


def shares(rows_ref, table_ref, head):
    rows = rows_ref[...]
    weights = jnp.zeros(rows.shape, F32)
    for c in range(table_ref.shape[0]):
        weights = jnp.where(rows == c, table_ref[c, head], weights)
    return weights / jnp.sum(weights, axis=0, keepdims=True)


def local_kernel(count, place_ref, table_ref, *refs):
    ks, qs = refs[:count], refs[count : 2 * count]
    v_ref, rows_ref, acc_ref, share_ref, q_all, k_all, k_t, sc = refs[2 * count :]
    tokens = q_all.shape[0]
    groups = tokens // GROUP

    @pl.when(pl.program_id(0) == 0)
    def _():
        place(ks, place_ref[0], k_all)
        place(qs, place_ref[0], q_all)
        k_t[...] = k_all[...].T
        row = lax.broadcasted_iota(jnp.int32, (GROUP, GROUP), 0)
        col = lax.broadcasted_iota(jnp.int32, (GROUP, GROUP), 1)
        for g in range(groups):
            at = slice(g * GROUP, (g + 1) * GROUP)
            own = dot(q_all[at, :], k_t[:, at])
            sc[at, GROUP:] = jnp.where(col <= row, own, 0.0)
            if g % 2 == 1:
                sc[at, :GROUP] = dot(q_all[at, :], k_t[:, (g - 1) * GROUP : g * GROUP])

    share = shares(rows_ref, table_ref, pl.program_id(0))
    share_ref[...] = share[None]
    share_t = share.T

    def scaled(value, at, level):
        return (value * share_t[at, level : level + 1]).astype(BF16)

    for g in range(groups):
        at = slice(g * GROUP, (g + 1) * GROUP)
        lhs = scaled(sc[at, GROUP:], at, 0)
        first = g
        if g % 2 == 1:
            lhs = jnp.concatenate([scaled(sc[at, :GROUP], at, 1), lhs], axis=1)
            first = g - 1
        acc_ref[at, :] = dot(lhs, v_ref[first * GROUP : (g + 1) * GROUP, :])
    pair = 2 * GROUP
    subtrees = [
        dot(k_t[:, p * pair : (p + 1) * pair], v_ref[p * pair : (p + 1) * pair, :])
        for p in range(groups // 2 - 1)
    ]
    half = pair
    level = 2
    while 2 * half <= tokens:
        for b in range(tokens // (2 * half)):
            at = slice((2 * b + 1) * half, (2 * b + 2) * half)
            left = subtrees[2 * b].astype(BF16)
            acc_ref[at, :] += dot(scaled(q_all[at, :].astype(F32), at, level), left)
        subtrees = [a + b for a, b in zip(subtrees[0::2], subtrees[1::2])]
        half *= 2
        level += 1


def far_kernel(count, bits, first_level, place_ref, *refs):
    qs = refs[:count]
    states = refs[count : count + bits]
    share_ref, acc_ref, out_ref, q_all = refs[count + bits :]

    @pl.when(pl.program_id(0) == 0)
    def _():
        place(qs, place_ref[0], q_all)

    share_t = share_ref[0].T
    q = q_all[...].astype(F32)
    parts = []
    for b in range(bits):
        on = (place_ref[1] >> b & 1).astype(F32)
        s = share_t[:, first_level + b : first_level + b + 1] * on
        parts.append((q * s).astype(BF16))
    lhs = jnp.concatenate(parts, axis=1)
    rhs = jnp.concatenate([s[...] for s in states], axis=0)
    out_ref[...] = (acc_ref[...] + dot(lhs, rhs)).astype(BF16)


def local(queries, keys, values, tier_weight_rows, level_table):
    tokens, columns = values.shape
    heads = level_table.shape[1]
    levels = tier_weight_rows.shape[0]
    width = columns // heads
    depth = keys.shape[1]
    rows = keys.shape[0]
    count = lax.axis_size("head")
    context_bits = lax.axis_size("ctx").bit_length() - 1
    local_bits = (tokens // GROUP).bit_length() - 1
    me = jnp.stack([lax.axis_index("head"), lax.axis_index("ctx")]).astype(jnp.int32)

    ks, qs = {0: keys}, {0: queries}
    bit = count // 2
    while bit:
        for held in (ks, qs):
            held.update({j | bit: exchanged(piece, "head", bit) for j, piece in held.items()})
        bit //= 2
    ks = [ks[j] for j in range(count)]
    qs = [qs[j] for j in range(count)]

    wide = min(columns, 2 * width)
    whole = pl.BlockSpec((rows, depth), lambda i, *_: (0, 0))
    column = pl.BlockSpec((tokens, width), lambda i, *_: (0, i))
    state_column = pl.BlockSpec((depth, width), lambda i, *_: (0, i))
    share_spec = pl.BlockSpec((1, levels, tokens), lambda i, *_: (i, 0, 0))
    params = pltpu.CompilerParams(
        dimension_semantics=("arbitrary",), vmem_limit_bytes=32 * 2**20
    )
    total, total_b = pl.pallas_call(
        functools.partial(state_kernel, count),
        out_shape=(
            jax.ShapeDtypeStruct((depth, columns), F32),
            jax.ShapeDtypeStruct((depth, columns), BF16),
        ),
        grid_spec=pltpu.PrefetchScalarGridSpec(
            num_scalar_prefetch=1,
            grid=(columns // wide,),
            in_specs=[whole] * count + [pl.BlockSpec((tokens, wide), lambda i, *_: (0, i))],
            out_specs=[pl.BlockSpec((depth, wide), lambda i, *_: (0, i))] * 2,
            scratch_shapes=[pltpu.VMEM((tokens, depth), BF16), pltpu.VMEM((depth, tokens), BF16)],
        ),
        compiler_params=params,
        name="state",
    )(me, *ks, values)

    states = []
    for b in range(context_bits):
        mask = 2 ** (b + 1) - 2 if b else 1
        incoming = exchanged(total_b, "ctx", mask)
        states.append(incoming)
        if b + 1 < context_bits:
            total = total + incoming.astype(F32)
            total_b = total.astype(BF16)

    acc, share = pl.pallas_call(
        functools.partial(local_kernel, count),
        out_shape=(
            jax.ShapeDtypeStruct((tokens, columns), F32),
            jax.ShapeDtypeStruct((heads, levels, tokens), F32),
        ),
        grid_spec=pltpu.PrefetchScalarGridSpec(
            num_scalar_prefetch=2,
            grid=(heads,),
            in_specs=[whole] * (2 * count)
            + [column, pl.BlockSpec((levels, tokens), lambda i, *_: (0, 0))],
            out_specs=[column, share_spec],
            scratch_shapes=[
                pltpu.VMEM((tokens, depth), BF16),
                pltpu.VMEM((tokens, depth), BF16),
                pltpu.VMEM((depth, tokens), BF16),
                pltpu.VMEM((tokens, 2 * GROUP), F32),
            ],
        ),
        compiler_params=params,
        cost_estimate=pl.CostEstimate(
            flops=8 * tokens * depth * columns, transcendentals=0, bytes_accessed=14 * tokens * columns
        ),
        name="near",
    )(me, level_table, *ks, *qs, values, tier_weight_rows)

    return pl.pallas_call(
        functools.partial(far_kernel, count, context_bits, 1 + local_bits),
        out_shape=jax.ShapeDtypeStruct((tokens, columns), BF16),
        grid_spec=pltpu.PrefetchScalarGridSpec(
            num_scalar_prefetch=1,
            grid=(heads,),
            in_specs=[whole] * count + [state_column] * context_bits + [share_spec, column],
            out_specs=column,
            scratch_shapes=[pltpu.VMEM((tokens, depth), BF16)],
        ),
        compiler_params=params,
        name="far",
    )(me, *qs, *states, share, acc)


def solution(mesh):
    placed = (
        P(("ctx", "head"), None),
        P(("ctx", "head"), None),
        P("ctx", "head"),
        P(None, "ctx"),
        P(None, "head"),
    )
    return jax.shard_map(
        local, mesh=mesh, in_specs=placed, out_specs=P("ctx", "head"), check_vma=False
    )
```

```python
import functools

import jax
import jax.numpy as jnp
from jax import lax
from jax.experimental import pallas as pl
from jax.experimental.pallas import tpu as pltpu
from jax.sharding import PartitionSpec as P


GROUP = 128
LANES = 128
F32 = jnp.float32
BF16 = jnp.bfloat16
VMEM = pl.BlockSpec(memory_space=pltpu.VMEM)
SMEM = pl.BlockSpec(memory_space=pltpu.SMEM)
HBM = pl.BlockSpec(memory_space=pltpu.HBM)


def exchanged(value, axis, mask):
    pairs = [(source, source ^ mask) for source in range(lax.axis_size(axis))]
    return lax.ppermute(value, axis, pairs)


def dot(a, b):
    return jnp.dot(a, b, preferred_element_type=F32)


def piece_rows(me, j, rows):
    return pl.ds(pl.multiple_of((me ^ j) * rows, rows), rows)


def split_shares(rows_ref, table_ref, heads):
    rows = rows_ref[...]
    levels, tokens = rows.shape
    hits = [rows == c for c in range(table_ref.shape[0])]
    found = []
    for head in range(heads):
        weights = jnp.zeros(rows.shape, F32)
        for c, hit in enumerate(hits):
            weights = jnp.where(hit, table_ref[c, head], weights)
        found.append(weights / jnp.sum(weights, axis=0, keepdims=True))
    share = jnp.concatenate(found, axis=0)
    high = share.astype(BF16).astype(F32)
    low = share - high
    spare = -2 * heads * levels % LANES
    parts = [high, low]
    if spare:
        parts.append(jnp.zeros((spare, tokens), F32))
    return jnp.concatenate(parts, axis=0).astype(BF16)


def early_kernel(early, heads, me_ref, table_ref, *refs):
    ks = refs[: early - 1]
    rows_hbm, q_hbm, k_hbm, v_hbm, q_out, k_out, v_out, s_ref, share_ref, rows_ref, sems = refs[
        early - 1 :
    ]
    me = me_ref[0]
    rows = k_out.shape[0]
    count = v_out.shape[0] // rows
    small = [
        pltpu.make_async_copy(source, target, sems.at[count + n])
        for n, (source, target) in enumerate(
            ((rows_hbm, rows_ref), (k_hbm, k_out), (q_hbm, q_out))
        )
    ]
    copies = []
    for j in range(count):
        at = piece_rows(me, j, rows)
        copies.append(pltpu.make_async_copy(v_hbm.at[at, :], v_out.at[at, :], sems.at[j]))
    for copy in small + copies:
        copy.start()
    small[0].wait()
    share_ref[...] = split_shares(rows_ref, table_ref, heads).T
    small[1].wait()
    small[2].wait()
    for j in range(early):
        copies[j].wait()
        k = ks[j - 1] if j else k_out
        part = dot(k[...].T, v_out[piece_rows(me, j, rows), :])
        s_ref[...] = part if j == 0 else s_ref[...] + part
    for j in range(early, count):
        copies[j].wait()


def state_kernel(which, me_ref, *refs):
    ks = refs[: len(which)]
    v_ref, before_ref, s_ref, b_ref = refs[len(which) :]
    rows = ks[0].shape[0]
    s = before_ref[...]
    for j, k in zip(which, ks):
        s = s + dot(k[...].T, v_ref[piece_rows(me_ref[0], j, rows), :])
    s_ref[...] = s
    b_ref[...] = s.astype(BF16)


def chooser(kinds, heads, levels, chunk, wide, level):
    row = lax.broadcasted_iota(jnp.int32, (kinds, wide), 0)
    col = lax.broadcasted_iota(jnp.int32, (kinds, wide), 1)
    width = wide // chunk[1]
    target = (chunk[0] * chunk[1] + col // width) * levels + level
    hit = (row == target) | (row == target + heads * levels)
    return jnp.where(hit, 1.0, 0.0).astype(BF16)


def local_kernel(count, heads, levels, me_ref, *refs):
    ks, qs = refs[:count], refs[count : 2 * count]
    v_ref, share_ref, acc_ref, q_all, k_t, sc = refs[2 * count :]
    tokens, columns = v_ref.shape
    groups = tokens // GROUP
    rows = ks[0].shape[0]
    width = columns // heads
    span = 2 if heads % 2 == 0 else 1
    wide = span * width
    kinds = share_ref.shape[1]
    me = me_ref[0]
    for j in range(count):
        q_all[piece_rows(me, j, rows), :] = qs[j][...]
        k_t[:, piece_rows(me, j, rows)] = ks[j][...].T
    row = lax.broadcasted_iota(jnp.int32, (GROUP, GROUP), 0)
    col = lax.broadcasted_iota(jnp.int32, (GROUP, GROUP), 1)
    for g in range(groups):
        at = slice(g * GROUP, (g + 1) * GROUP)
        own = dot(q_all[at, :], k_t[:, at])
        sc[at, GROUP:] = jnp.where(col <= row, own, 0.0).astype(BF16)
        if g % 2 == 1:
            before = slice((g - 1) * GROUP, g * GROUP)
            sc[at, :GROUP] = dot(q_all[at, :], k_t[:, before]).astype(BF16)

    @pl.loop(0, columns // wide)
    def _(i):
        cs = pl.ds(pl.multiple_of(i * wide, wide), wide)

        def choose(level):
            return chooser(kinds, heads, levels, (i, span), wide, level)

        own_level, pair_level = choose(0), choose(1)
        for g in range(groups):
            at = slice(g * GROUP, (g + 1) * GROUP)
            part = dot(share_ref[at, :], own_level) * dot(sc[at, GROUP:], v_ref[at, cs])
            if g % 2 == 1:
                before = slice((g - 1) * GROUP, g * GROUP)
                part = part + dot(share_ref[at, :], pair_level) * dot(
                    sc[at, :GROUP], v_ref[before, cs]
                )
            acc_ref[at, cs] = part
        pair = 2 * GROUP
        subtrees = [
            dot(k_t[:, p * pair : (p + 1) * pair], v_ref[p * pair : (p + 1) * pair, cs])
            for p in range(groups // 2 - 1)
        ]
        half = pair
        level = 2
        while 2 * half <= tokens:
            chosen = choose(level)
            step = min(half, 512)
            for b in range(tokens // (2 * half)):
                left = subtrees[2 * b].astype(BF16)
                for first in range((2 * b + 1) * half, (2 * b + 2) * half, step):
                    at = slice(first, first + step)
                    acc_ref[at, cs] += dot(share_ref[at, :], chosen) * dot(q_all[at, :], left)
            subtrees = [a + b for a, b in zip(subtrees[0::2], subtrees[1::2])]
            half *= 2
            level += 1


def far_parts(heads, levels, level, bit, me_ref, q_ref, share_ref, state_ref, i, wide, span):
    on = (me_ref[1] >> bit & 1) == 1
    chosen = chooser(share_ref.shape[1], heads, levels, (i, span), wide, level)
    chosen = jnp.where(on, chosen, jnp.zeros_like(chosen))
    cs = pl.ds(pl.multiple_of(i * wide, wide), wide)
    state = state_ref[:, cs]
    tokens = q_ref.shape[0]
    step = min(tokens, 512)
    for first in range(0, tokens, step):
        at = slice(first, first + step)
        yield at, cs, dot(share_ref[at, :], chosen) * dot(q_ref[at, :], state)


def spans(heads, columns):
    span = 2 if heads % 2 == 0 else 1
    return span, span * columns // heads


def middle_kernel(heads, levels, level, bit, me_ref, q_ref, share_ref, state_ref, acc_ref, out_ref):
    span, wide = spans(heads, state_ref.shape[1])

    @pl.loop(0, heads // span)
    def _(i):
        for at, cs, part in far_parts(
            heads, levels, level, bit, me_ref, q_ref, share_ref, state_ref, i, wide, span
        ):
            out_ref[at, cs] = acc_ref[at, cs] + part


def last_kernel(
    heads, levels, level, bit, me_ref, q_ref, share_ref, state_ref, acc_ref, out_ref, buf, sems
):
    span, wide = spans(heads, state_ref.shape[1])
    copies = []
    for i in range(heads // span):
        for at, cs, part in far_parts(
            heads, levels, level, bit, me_ref, q_ref, share_ref, state_ref, i, wide, span
        ):
            at_cols = slice(i * wide, (i + 1) * wide)
            buf[at, at_cols] = (acc_ref[at, at_cols] + part).astype(BF16)
        cols = pl.ds(i * wide, wide)
        copies.append(pltpu.make_async_copy(buf.at[:, cols], out_ref.at[:, cols], sems.at[i]))
        copies[-1].start()
    for copy in copies:
        copy.wait()


def layer(queries, keys, values, tier_weight_rows, level_table):
    tokens, columns = values.shape
    heads = level_table.shape[1]
    levels = tier_weight_rows.shape[0]
    depth = keys.shape[1]
    rows = keys.shape[0]
    count = lax.axis_size("head")
    context_bits = lax.axis_size("ctx").bit_length() - 1
    local_bits = (tokens // GROUP).bit_length() - 1
    kinds = pl.cdiv(2 * heads * levels, LANES) * LANES
    me = jnp.stack([lax.axis_index("head"), lax.axis_index("ctx")]).astype(jnp.int32)

    ks, qs = {0: keys}, {0: queries}
    bit = count // 2
    while bit:
        for held in (ks, qs):
            for j, piece in list(held.items()):
                held[j | bit] = exchanged(piece, "head", bit)
        bit //= 2
    ks = [ks[j] for j in range(count)]
    qs = [qs[j] for j in range(count)]

    def shape(*dims, dtype=F32):
        return jax.ShapeDtypeStruct(dims, dtype)

    def cost(flops):
        return pl.CostEstimate(
            flops=flops * tokens * depth * columns, transcendentals=0, bytes_accessed=2 * tokens * columns
        )

    params = pltpu.CompilerParams(vmem_limit_bytes=24 * 2**20)
    early = max(1, count // 2)
    fixed = [
        pltpu.with_memory_space_constraint(a, pltpu.HBM)
        for a in (tier_weight_rows, queries, keys, values)
    ]
    qs[0], ks[0], held, total, share = pl.pallas_call(
        functools.partial(early_kernel, early, heads),
        out_shape=(
            shape(rows, depth, dtype=BF16),
            shape(rows, depth, dtype=BF16),
            shape(tokens, columns, dtype=BF16),
            shape(depth, columns),
            shape(tokens, kinds, dtype=BF16),
        ),
        in_specs=[SMEM, SMEM] + [VMEM] * (early - 1) + [HBM] * 4,
        out_specs=(VMEM,) * 5,
        scratch_shapes=[
            pltpu.VMEM((levels, tokens), jnp.int32),
            pltpu.SemaphoreType.DMA((count + 3,)),
        ],
        compiler_params=params,
        cost_estimate=cost(1),
        name="early",
    )(me, level_table, *ks[1:early], *fixed)

    total_b = total.astype(BF16)
    for which in (range(early, count - 1), range(count - 1, count)):
        which = [j for j in which if j >= early]
        if not which:
            continue
        total, total_b = pl.pallas_call(
            functools.partial(state_kernel, which),
            out_shape=(shape(depth, columns), shape(depth, columns, dtype=BF16)),
            in_specs=[SMEM] + [VMEM] * (len(which) + 2),
            out_specs=(VMEM, VMEM),
            compiler_params=params,
            name="state",
        )(me, *[ks[j] for j in which], held, total)

    states = []
    for b in range(context_bits):
        mask = 2 ** (b + 1) - 2 if b else 1
        incoming = exchanged(total_b, "ctx", mask)
        states.append(incoming)
        if b + 1 < context_bits:
            total = total + incoming.astype(F32)
            total_b = total.astype(BF16)

    acc, q_all = pl.pallas_call(
        functools.partial(local_kernel, count, heads, levels),
        out_shape=(shape(tokens, columns), shape(tokens, depth, dtype=BF16)),
        in_specs=[SMEM] + [VMEM] * (2 * count + 2),
        out_specs=(VMEM, VMEM),
        scratch_shapes=[pltpu.VMEM((depth, tokens), BF16), pltpu.VMEM((tokens, 2 * GROUP), BF16)],
        compiler_params=params,
        cost_estimate=cost(4),
        name="near",
    )(me, *ks, *qs, held, share)

    for b in range(context_bits - 1):
        acc = pl.pallas_call(
            functools.partial(middle_kernel, heads, levels, 1 + local_bits + b, b),
            out_shape=shape(tokens, columns),
            in_specs=[SMEM] + [VMEM] * 4,
            out_specs=VMEM,
            input_output_aliases={4: 0},
            compiler_params=params,
            cost_estimate=cost(2),
        )(me, q_all, share, states[b], acc)

    b = context_bits - 1
    span, _ = spans(heads, columns)
    return pl.pallas_call(
        functools.partial(last_kernel, heads, levels, 1 + local_bits + b, b),
        out_shape=shape(tokens, columns, dtype=BF16),
        in_specs=[SMEM] + [VMEM] * 4,
        out_specs=HBM,
        scratch_shapes=[
            pltpu.VMEM((tokens, columns), BF16),
            pltpu.SemaphoreType.DMA((heads // span,)),
        ],
        compiler_params=params,
        name="last",
    )(me, q_all, share, states[b], acc)


def solution(mesh):
    placed = (
        P(("ctx", "head"), None),
        P(("ctx", "head"), None),
        P("ctx", "head"),
        P(None, "ctx"),
        P(None, "head"),
    )
    return jax.shard_map(
        layer, mesh=mesh, in_specs=placed, out_specs=P("ctx", "head"), check_vma=False
    )
```

```python
import functools

import jax
import jax.numpy as jnp
from jax import lax
from jax.experimental import pallas as pl
from jax.experimental.pallas import tpu as pltpu
from jax.sharding import PartitionSpec as P


GROUP = 128
F32 = jnp.float32
BF16 = jnp.bfloat16
CHAIN = 2
VMEM = pl.BlockSpec(memory_space=pltpu.VMEM)
SMEM = pl.BlockSpec(memory_space=pltpu.SMEM)
HBM = pl.BlockSpec(memory_space=pltpu.HBM)


def exchanged(value, axis, mask):
    pairs = [(source, source ^ mask) for source in range(lax.axis_size(axis))]
    return lax.ppermute(value, axis, pairs)


def dot(a, b):
    return jnp.dot(a, b, preferred_element_type=F32)


def piece_rows(me, j, rows):
    return pl.ds(pl.multiple_of((me ^ j) * rows, rows), rows)


def store_shares(rows_ref, table_ref, share_ref):
    rows = rows_ref[...]
    hits = [rows == c for c in range(table_ref.shape[1])]
    for head in range(share_ref.shape[0]):
        weights = jnp.zeros(rows.shape, F32)
        for c, hit in enumerate(hits):
            weights = jnp.where(hit, table_ref[head, c], weights)
        share_ref[head] = weights / jnp.sum(weights, axis=0, keepdims=True)


def add_pairs(k_ref, v_ref, pairs_ref, j):
    rows = k_ref.shape[0]
    pair = 2 * GROUP
    me = lax.axis_index("head") ^ j
    k_t = k_ref[...].T
    total = None
    for r in range(rows // pair):
        start = pl.multiple_of(me * rows + r * pair, pair)
        part = dot(k_t[:, r * pair : (r + 1) * pair], v_ref[pl.ds(start, pair), :])
        pairs_ref[me * (rows // pair) + r] = part
        total = part if total is None else total + part
    return total


def early_kernel(table_ref, rows_hbm, q_hbm, k_hbm, v_hbm, *refs):
    q_out, k_out, v_out, s_ref, pairs_ref, share_ref, rows_ref, sems = refs
    me = lax.axis_index("head")
    rows = k_out.shape[0]
    count = v_out.shape[0] // rows
    small = [
        pltpu.make_async_copy(source, target, sems.at[count + n])
        for n, (source, target) in enumerate(
            ((rows_hbm, rows_ref), (k_hbm, k_out), (q_hbm, q_out))
        )
    ]
    copies = []
    for j in range(count):
        at = piece_rows(me, j, rows)
        copies.append(pltpu.make_async_copy(v_hbm.at[at, :], v_out.at[at, :], sems.at[j]))
    for copy in small + copies:
        copy.start()
    small[0].wait()
    store_shares(rows_ref, table_ref, share_ref)
    small[1].wait()
    small[2].wait()
    copies[0].wait()
    s_ref[...] = add_pairs(k_out, v_out, pairs_ref, 0)
    for copy in copies[1:]:
        copy.wait()


def state_kernel(which, *refs):
    ks = refs[: len(which)]
    v_ref, before_ref, _ = refs[len(which) : len(which) + 3]
    pairs_ref, *outs = refs[len(which) + 3 :]
    s = before_ref[...]
    for j, k in zip(which, ks):
        s = s + add_pairs(k, v_ref, pairs_ref, j)
    if len(outs) == 1:
        outs[0][...] = s
        return
    width = outs[0].shape[1]
    for c in range(len(outs) // 2):
        part = s[:, c * width : (c + 1) * width]
        outs[2 * c][...] = part
        outs[2 * c + 1][...] = part.astype(BF16)


def score_kernel(count, *refs):
    ks, qs = refs[:count], refs[count : 2 * count]
    q_t, q_f, scores, k_all = refs[2 * count :]
    pair = scores.shape[1]
    for j in range(count):
        at = piece_rows(lax.axis_index("head"), j, ks[0].shape[0])
        k_all[at, :] = ks[j][...]
        turned_q = qs[j][...].T
        q_t[:, at] = turned_q
        q_f[:, at] = turned_q.astype(F32)
    source = lax.broadcasted_iota(jnp.int32, (pair, pair), 0)
    token = lax.broadcasted_iota(jnp.int32, (pair, pair), 1)
    for p in range(scores.shape[0] // pair):
        at = slice(p * pair, (p + 1) * pair)
        scores[at, :] = jnp.where(source <= token, dot(k_all[at, :], q_t[:, at]), 0.0)


def loop_heads(heads, body):
    unroll = 2 if heads % 2 == 0 else 1

    @pl.loop(0, heads // unroll)
    def _(i):
        for n in range(unroll):
            body(i * unroll + n)


def near_kernel(base, width, v_ref, pairs_ref, q_ref, scores_ref, share_ref, acc_ref):
    tokens, pair = scores_ref.shape
    group = pair // 2
    pairs = tokens // pair

    def head(i):
        h = base + i
        cols = pl.ds(pl.multiple_of(h * width, width), width)
        outs = pl.ds(pl.multiple_of(i * width, width), width)
        older = lax.broadcasted_iota(jnp.int32, (1, pair), 1) < group
        uses = [[] for _ in range(pairs)]
        subtrees = [pairs_ref[p, :, cols] for p in range(pairs - 1)]
        level, size = 2, 1
        while 2 * size <= pairs:
            for b in range(0, pairs // size, 2):
                left = subtrees[b].astype(BF16).T
                for p in range((b + 1) * size, (b + 2) * size):
                    uses[p].append((level, left))
            subtrees = [x + y for x, y in zip(subtrees[0::2], subtrees[1::2])]
            level, size = level + 1, 2 * size
        for p, used in enumerate(uses):
            at = slice(p * pair, (p + 1) * pair)
            first = slice(p * pair, p * pair + group)
            second = slice(p * pair + group, (p + 1) * pair)
            own = share_ref[h, 0:1, at]
            above = jnp.where(older, own, share_ref[h, 1:2, at])
            top = (scores_ref[first, :] * above).astype(BF16)
            low = (scores_ref[second, group:] * own[:, group:]).astype(BF16)
            bottom = jnp.concatenate([jnp.zeros((group, group), BF16), low], axis=1)
            lhs, rhs = [v_ref[at, cols].T], [top, bottom]
            for l, left in used:
                lhs.append(left)
                rhs.append((q_ref[:, at] * share_ref[h, l : l + 1, at]).astype(BF16))
            acc_ref[outs, at] = dot(jnp.concatenate(lhs, axis=1), jnp.concatenate(rhs, axis=0))

    loop_heads(acc_ref.shape[0] // width, head)


def lit(share_ref, h, level, bit, at):
    share = share_ref[h, level : level + 1, at]
    return jnp.where((lax.axis_index("ctx") >> bit & 1) == 1, share, jnp.zeros_like(share))


def middle_kernel(levels, base, width, q_ref, share_ref, *refs):
    states, (acc_ref, out_ref) = refs[:-2], refs[-2:]
    rows, tokens = acc_ref.shape
    step = min(tokens, 2 * GROUP)

    def head(i):
        cols = pl.ds(pl.multiple_of(i * width, width), width)
        lhs = jnp.concatenate([state[:, cols].T for state in states], axis=1)
        for first in range(0, tokens, step):
            at = slice(first, first + step)
            rhs = [
                (q_ref[:, at] * lit(share_ref, base + i, level, bit, at)).astype(BF16)
                for level, bit in levels
            ]
            out_ref[cols, at] = acc_ref[cols, at] + dot(lhs, jnp.concatenate(rhs, axis=0))

    loop_heads(rows // width, head)


def last_kernel(level, bit, base, width, q_ref, share_ref, state_ref, acc_ref, *refs):
    out_ref, buf, sems = refs[-3:]
    rows, tokens = acc_ref.shape
    step = min(tokens, 2 * GROUP)
    lhs = state_ref[...].T
    copies = []
    for n, first in enumerate(range(0, tokens, step)):
        at = slice(first, first + step)
        found = dot(lhs, q_ref[:, at])
        for i in range(rows // width):
            cols = slice(i * width, (i + 1) * width)
            part = lit(share_ref, base + i, level, bit, at) * found[cols, :]
            buf[at, cols] = (acc_ref[cols, at] + part).astype(BF16).T
        target = out_ref.at[at, pl.ds(base * width, rows)]
        copies.append(pltpu.make_async_copy(buf.at[at, :], target, sems.at[n]))
        copies[-1].start()
    for copy in copies:
        copy.wait()


def chunks(heads):
    return CHAIN if heads % CHAIN == 0 else 1


def layer(queries, keys, values, tier_weight_rows, level_table):
    tokens, columns = values.shape
    heads = level_table.shape[1]
    levels = tier_weight_rows.shape[0]
    width = columns // heads
    rows, depth = keys.shape
    count = lax.axis_size("head")
    context_bits = lax.axis_size("ctx").bit_length() - 1
    local_bits = (tokens // GROUP).bit_length() - 1
    chain = chunks(heads)
    part = columns // chain
    ks, qs = {0: keys}, {0: queries}
    bit = count // 2
    while bit:
        for held in (ks, qs):
            for j, piece in list(held.items()):
                held[j | bit] = exchanged(piece, "head", bit)
        bit //= 2
    ks = [ks[j] for j in range(count)]
    qs = [qs[j] for j in range(count)]

    def shape(*dims, dtype=F32):
        return jax.ShapeDtypeStruct(dims, dtype)

    def call(kernel, flops, *args, **kwargs):
        cost = pl.CostEstimate(
            flops=int(flops * tokens * depth * columns), transcendentals=0, bytes_accessed=tokens * columns
        )
        return pl.pallas_call(
            kernel,
            cost_estimate=cost,
            compiler_params=pltpu.CompilerParams(vmem_limit_bytes=24 * 2**20),
            **kwargs,
        )(*args)

    fixed = [
        pltpu.with_memory_space_constraint(a, pltpu.HBM)
        for a in (tier_weight_rows, queries, keys, values)
    ]
    pair_states = shape(tokens // (2 * GROUP), depth, columns)
    qs[0], ks[0], held, total, pair_sums, share = call(
        early_kernel,
        1,
        level_table.T,
        *fixed,
        out_shape=(
            shape(rows, depth, dtype=BF16),
            shape(rows, depth, dtype=BF16),
            shape(tokens, columns, dtype=BF16),
            shape(depth, columns),
            pair_states,
            shape(heads, levels, tokens),
        ),
        in_specs=[SMEM] + [HBM] * 4,
        out_specs=(VMEM,) * 6,
        scratch_shapes=[
            pltpu.VMEM((levels, tokens), jnp.int32),
            pltpu.SemaphoreType.DMA((count + 3,)),
        ],
    )
    split = (shape(depth, part), shape(depth, part, dtype=BF16)) * chain
    half = max(1, count // 2)
    order = list(range(count))
    steps = [w for w in (order[1:half], order[half:-1], order[-1:]) if w]
    for n, which in enumerate(steps):
        outs = split if n == len(steps) - 1 else (shape(depth, columns),)
        pair_sums, *total = call(
            functools.partial(state_kernel, which),
            0.5,
            *[ks[j] for j in which],
            held,
            total,
            pair_sums,
            out_shape=(pair_states, *outs),
            in_specs=[VMEM] * (len(which) + 3),
            out_specs=(VMEM,) * (1 + len(outs)),
            input_output_aliases={len(which) + 2: 0},
        )
        total = total[0] if len(total) == 1 else total
    sums = [total[2 * c] for c in range(chain)]
    sent = [total[2 * c + 1] for c in range(chain)]

    states = [[] for _ in range(chain)]
    for b in range(context_bits):
        mask = 2 ** (b + 1) - 2 if b else 1
        for c in range(chain):
            incoming = exchanged(sent[c], "ctx", mask)
            states[c].append(incoming)
            if b + 1 < context_bits:
                sums[c] = sums[c] + incoming.astype(F32)
                sent[c] = sums[c].astype(BF16)

    q_t, q_f, scores = call(
        functools.partial(score_kernel, count),
        0.3,
        *ks,
        *qs,
        out_shape=(
            shape(depth, tokens, dtype=BF16),
            shape(depth, tokens),
            shape(tokens, 2 * GROUP),
        ),
        in_specs=[VMEM] * (2 * count),
        out_specs=(VMEM,) * 3,
        scratch_shapes=[pltpu.VMEM((tokens, depth), BF16)],
    )
    accs = [
        call(
            functools.partial(near_kernel, c * heads // chain, width),
            4 / chain,
            held,
            pair_sums,
            q_f,
            scores,
            share,
            out_shape=shape(part, tokens),
            in_specs=[VMEM] * 5,
            out_specs=VMEM,
        )
        for c in range(chain)
    ]
    places = [(1 + local_bits + b, b) for b in range(context_bits)]
    for c in range(chain):
        accs[c] = call(
            functools.partial(middle_kernel, places[:-1], c * heads // chain, width),
            2 / chain,
            q_f,
            share,
            *states[c][:-1],
            accs[c],
            out_shape=shape(part, tokens),
            in_specs=[VMEM] * (context_bits + 2),
            out_specs=VMEM,
            input_output_aliases={context_bits + 1: 0},
        )
    out = []
    for c in range(chain):
        out = [
            call(
                functools.partial(last_kernel, *places[-1], c * heads // chain, width),
                1 / chain,
                q_t,
                share,
                states[c][-1],
                accs[c],
                *out,
                out_shape=shape(tokens, columns, dtype=BF16),
                in_specs=[VMEM] * 4 + [HBM] * len(out),
                out_specs=HBM,
                input_output_aliases={4: 0} if out else {},
                scratch_shapes=[
                    pltpu.VMEM((tokens, part), BF16),
                    pltpu.SemaphoreType.DMA((tokens // (2 * GROUP),)),
                ],
            )
        ]
    return out[0]


def solution(mesh):
    placed = (
        P(("ctx", "head"), None),
        P(("ctx", "head"), None),
        P("ctx", "head"),
        P(None, "ctx"),
        P(None, "head"),
    )
    return jax.shard_map(
        layer, mesh=mesh, in_specs=placed, out_specs=P("ctx", "head"), check_vma=False
    )
```

```python
import functools

import jax
import jax.numpy as jnp
from jax import lax
from jax.experimental import pallas as pl
from jax.experimental.pallas import tpu as pltpu
from jax.sharding import PartitionSpec as P


GROUP = 128
F32 = jnp.float32
BF16 = jnp.bfloat16
VMEM = pl.BlockSpec(memory_space=pltpu.VMEM)
HBM = pl.BlockSpec(memory_space=pltpu.HBM)


def exchanged(value, axis, mask):
    pairs = [(source, source ^ mask) for source in range(lax.axis_size(axis))]
    return lax.ppermute(value, axis, pairs)


def dot(a, b):
    return jnp.dot(a, b, preferred_element_type=F32)


def piece_rows(me, j, rows):
    return pl.ds(pl.multiple_of((me ^ j) * rows, rows), rows)


def store_shares(rows_ref, table_ref, share_ref):
    rows = rows_ref[...]
    hits = [rows == c for c in range(table_ref.shape[1])]
    for head in range(share_ref.shape[0]):
        weights = jnp.zeros(rows.shape, F32)
        for c, hit in enumerate(hits):
            weights = jnp.where(hit, table_ref[head, c], weights)
        share_ref[head] = weights / jnp.sum(weights, axis=0, keepdims=True)


def add_pairs(k_ref, v_ref, pairs_ref, j):
    rows = k_ref.shape[0]
    pair = 2 * GROUP
    me = lax.axis_index("head") ^ j
    k_t = k_ref[...].T
    total = None
    for r in range(rows // pair):
        start = pl.multiple_of(me * rows + r * pair, pair)
        part = dot(k_t[:, r * pair : (r + 1) * pair], v_ref[pl.ds(start, pair), :])
        pairs_ref[me * (rows // pair) + r] = part
        total = part if total is None else total + part
    return total


def early_kernel(table_hbm, rows_hbm, q_hbm, k_hbm, v_hbm, *refs):
    q_out, k_out, v_out, s_ref, pairs_ref, share_ref, rows_ref, table_ref, sems = refs
    me = lax.axis_index("head")
    rows = k_out.shape[0]
    count = v_out.shape[0] // rows
    small = [
        pltpu.make_async_copy(source, target, sems.at[count + n])
        for n, (source, target) in enumerate(
            ((rows_hbm, rows_ref), (table_hbm, table_ref), (k_hbm, k_out), (q_hbm, q_out))
        )
    ]
    copies = []
    for j in range(count):
        at = piece_rows(me, j, rows)
        copies.append(pltpu.make_async_copy(v_hbm.at[at, :], v_out.at[at, :], sems.at[j]))
    for copy in small + copies:
        copy.start()
    small[0].wait()
    small[1].wait()
    store_shares(rows_ref, table_ref, share_ref)
    small[2].wait()
    small[3].wait()
    copies[0].wait()
    s_ref[...] = add_pairs(k_out, v_out, pairs_ref, 0)
    for copy in copies[1:]:
        copy.wait()


def state_kernel(which, *refs):
    ks = refs[: len(which)]
    v_ref, before_ref, _ = refs[len(which) : len(which) + 3]
    pairs_ref, *outs = refs[len(which) + 3 :]
    s = before_ref[...]
    for j, k in zip(which, ks):
        s = s + add_pairs(k, v_ref, pairs_ref, j)
    if len(outs) == 1:
        outs[0][...] = s
        return
    first = 0
    for exact, rounded in zip(outs[0::2], outs[1::2]):
        part = s[:, first : first + exact.shape[1]]
        exact[...] = part
        rounded[...] = part.astype(BF16)
        first += exact.shape[1]


def score_kernel(count, *refs):
    ks, qs = refs[:count], refs[count : 2 * count]
    q_t, q_f, scores, k_all = refs[2 * count :]
    pair = scores.shape[1]
    for j in range(count):
        at = piece_rows(lax.axis_index("head"), j, ks[0].shape[0])
        k_all[at, :] = ks[j][...]
        turned_q = qs[j][...].T
        q_t[:, at] = turned_q
        q_f[:, at] = turned_q.astype(F32)
    source = lax.broadcasted_iota(jnp.int32, (pair, pair), 0)
    token = lax.broadcasted_iota(jnp.int32, (pair, pair), 1)
    for p in range(scores.shape[0] // pair):
        at = slice(p * pair, (p + 1) * pair)
        scores[at, :] = jnp.where(source <= token, dot(k_all[at, :], q_t[:, at]), 0.0)


def loop_heads(heads, body):
    for i in range(heads):
        body(i)


def near_kernel(base, width, v_ref, pairs_ref, q_ref, scores_ref, share_ref, acc_ref):
    tokens, pair = scores_ref.shape
    group = pair // 2
    pairs = tokens // pair

    def head(i):
        h = base + i
        cols = slice(h * width, (h + 1) * width)
        outs = slice(i * width, (i + 1) * width)
        older = lax.broadcasted_iota(jnp.int32, (1, pair), 1) < group
        uses = [[] for _ in range(pairs)]
        subtrees = [pairs_ref[p, :, cols] for p in range(pairs - 1)]
        level, size = 2, 1
        while 2 * size <= pairs:
            for b in range(0, pairs // size, 2):
                left = subtrees[b].astype(BF16).T
                for p in range((b + 1) * size, (b + 2) * size):
                    uses[p].append((level, left))
            subtrees = [x + y for x, y in zip(subtrees[0::2], subtrees[1::2])]
            level, size = level + 1, 2 * size
        for p, used in enumerate(uses):
            at = slice(p * pair, (p + 1) * pair)
            first = slice(p * pair, p * pair + group)
            second = slice(p * pair + group, (p + 1) * pair)
            own = share_ref[h, 0:1, at]
            above = jnp.where(older, own, share_ref[h, 1:2, at])
            top = (scores_ref[first, :] * above).astype(BF16)
            low = (scores_ref[second, group:] * own[:, group:]).astype(BF16)
            bottom = jnp.concatenate([jnp.zeros((group, group), BF16), low], axis=1)
            lhs, rhs = [v_ref[at, cols].T], [top, bottom]
            for l, left in used:
                lhs.append(left)
                rhs.append((q_ref[:, at] * share_ref[h, l : l + 1, at]).astype(BF16))
            acc_ref[outs, at] = dot(jnp.concatenate(lhs, axis=1), jnp.concatenate(rhs, axis=0))

    loop_heads(acc_ref.shape[0] // width, head)


def lit(share_ref, h, level, bit, at):
    share = share_ref[h, level : level + 1, at]
    return jnp.where((lax.axis_index("ctx") >> bit & 1) == 1, share, jnp.zeros_like(share))


def middle_kernel(levels, base, width, q_ref, share_ref, *refs):
    states, (acc_ref, out_ref) = refs[:-2], refs[-2:]
    rows, tokens = acc_ref.shape
    step = min(tokens, 2 * GROUP)

    def head(i):
        cols = slice(i * width, (i + 1) * width)
        lhs = jnp.concatenate([state[:, cols].T for state in states], axis=1)
        for first in range(0, tokens, step):
            at = slice(first, first + step)
            rhs = [
                (q_ref[:, at] * lit(share_ref, base + i, level, bit, at)).astype(BF16)
                for level, bit in levels
            ]
            out_ref[cols, at] = acc_ref[cols, at] + dot(lhs, jnp.concatenate(rhs, axis=0))

    @pl.when((lax.axis_index("ctx") & sum(1 << bit for _, bit in levels)) != 0)
    def _():
        loop_heads(rows // width, head)


def last_kernel(level, bit, base, width, q_ref, share_ref, state_ref, acc_ref, *refs):
    out_ref, buf, sems = refs[-3:]
    rows, tokens = acc_ref.shape
    step = min(tokens, 2 * GROUP)
    copies = [
        pltpu.make_async_copy(
            buf.at[first : first + step, :],
            out_ref.at[first : first + step, pl.ds(base * width, rows)],
            sems.at[n],
        )
        for n, first in enumerate(range(0, tokens, step))
    ]

    def finish(reached):
        if reached:
            lhs = state_ref[...].T
        for copy, first in zip(copies, range(0, tokens, step)):
            at = slice(first, first + step)
            if reached:
                found = dot(lhs, q_ref[:, at])
            for i in range(rows // width):
                cols = slice(i * width, (i + 1) * width)
                total = acc_ref[cols, at]
                if reached:
                    total = total + share_ref[base + i, level : level + 1, at] * found[cols, :]
                buf[at, cols] = total.astype(BF16).T
            copy.start()

    on = (lax.axis_index("ctx") >> bit & 1) == 1
    pl.when(on)(functools.partial(finish, True))
    pl.when(jnp.logical_not(on))(functools.partial(finish, False))
    for copy in copies:
        copy.wait()


def chunks(heads):
    small = max(1, 3 * heads // 8)
    return ((0, small), (small, heads)) if heads > 1 else ((0, 1),)


def layer(queries, keys, values, tier_weight_rows, level_table):
    tokens, columns = values.shape
    heads = level_table.shape[1]
    levels = tier_weight_rows.shape[0]
    width = columns // heads
    rows, depth = keys.shape
    count = lax.axis_size("head")
    context_bits = lax.axis_size("ctx").bit_length() - 1
    local_bits = (tokens // GROUP).bit_length() - 1
    spans = chunks(heads)
    chain = len(spans)
    parts = [(b - a) * width for a, b in spans]
    ks, qs = {0: keys}, {0: queries}
    bit = count // 2
    while bit:
        for held in (ks, qs):
            for j, piece in list(held.items()):
                held[j | bit] = exchanged(piece, "head", bit)
        bit //= 2
    ks = [ks[j] for j in range(count)]
    qs = [qs[j] for j in range(count)]

    def shape(*dims, dtype=F32):
        return jax.ShapeDtypeStruct(dims, dtype)

    def call(kernel, flops, *args, **kwargs):
        cost = pl.CostEstimate(
            flops=int(flops * tokens * depth * columns), transcendentals=0, bytes_accessed=tokens * columns
        )
        return pl.pallas_call(
            kernel,
            cost_estimate=cost,
            compiler_params=pltpu.CompilerParams(vmem_limit_bytes=24 * 2**20),
            **kwargs,
        )(*args)

    fixed = [
        pltpu.with_memory_space_constraint(a, pltpu.HBM)
        for a in (level_table.T, tier_weight_rows, queries, keys, values)
    ]
    pair_states = shape(tokens // (2 * GROUP), depth, columns)
    qs[0], ks[0], held, total, pair_sums, share = call(
        early_kernel,
        1,
        *fixed,
        out_shape=(
            shape(rows, depth, dtype=BF16),
            shape(rows, depth, dtype=BF16),
            shape(tokens, columns, dtype=BF16),
            shape(depth, columns),
            pair_states,
            shape(heads, levels, tokens),
        ),
        in_specs=[HBM] * 5,
        out_specs=(VMEM,) * 6,
        scratch_shapes=[
            pltpu.VMEM((levels, tokens), jnp.int32),
            pltpu.SMEM(level_table.T.shape, F32),
            pltpu.SemaphoreType.DMA((count + 4,)),
        ],
    )
    split = tuple(shape(depth, p, dtype=d) for p in parts for d in (F32, BF16))
    half = max(1, count // 2)
    order = list(range(count))
    steps = [w for w in (order[1:half], order[half:-1], order[-1:]) if w]
    for n, which in enumerate(steps):
        outs = split if n == len(steps) - 1 else (shape(depth, columns),)
        pair_sums, *total = call(
            functools.partial(state_kernel, which),
            0.5,
            *[ks[j] for j in which],
            held,
            total,
            pair_sums,
            out_shape=(pair_states, *outs),
            in_specs=[VMEM] * (len(which) + 3),
            out_specs=(VMEM,) * (1 + len(outs)),
            input_output_aliases={len(which) + 2: 0},
        )
        total = total[0] if len(total) == 1 else total
    sums = [total[2 * c] for c in range(chain)]
    sent = [total[2 * c + 1] for c in range(chain)]

    states = [[] for _ in range(chain)]
    for b in range(context_bits):
        mask = 2 ** (b + 1) - 2 if b else 1
        for c in range(chain):
            incoming = exchanged(sent[c], "ctx", mask)
            states[c].append(incoming)
            if b + 1 < context_bits:
                sums[c] = sums[c] + incoming.astype(F32)
                sent[c] = sums[c].astype(BF16)

    q_t, q_f, scores = call(
        functools.partial(score_kernel, count),
        0.3,
        *ks,
        *qs,
        out_shape=(
            shape(depth, tokens, dtype=BF16),
            shape(depth, tokens),
            shape(tokens, 2 * GROUP),
        ),
        in_specs=[VMEM] * (2 * count),
        out_specs=(VMEM,) * 3,
        scratch_shapes=[pltpu.VMEM((tokens, depth), BF16)],
    )
    accs = [
        call(
            functools.partial(near_kernel, spans[c][0], width),
            4 * parts[c] / columns,
            held,
            pair_sums,
            q_f,
            scores,
            share,
            out_shape=shape(parts[c], tokens),
            in_specs=[VMEM] * 5,
            out_specs=VMEM,
        )
        for c in range(chain)
    ]
    places = [(1 + local_bits + b, b) for b in range(context_bits)]
    for c in range(chain):
        accs[c] = call(
            functools.partial(middle_kernel, places[:-1], spans[c][0], width),
            2 * parts[c] / columns,
            q_f,
            share,
            *states[c][:-1],
            accs[c],
            out_shape=shape(parts[c], tokens),
            in_specs=[VMEM] * (context_bits + 2),
            out_specs=VMEM,
            input_output_aliases={context_bits + 1: 0},
        )
    out = []
    for c in range(chain):
        out = [
            call(
                functools.partial(last_kernel, *places[-1], spans[c][0], width),
                parts[c] / columns,
                q_t,
                share,
                states[c][-1],
                accs[c],
                *out,
                out_shape=shape(tokens, columns, dtype=BF16),
                in_specs=[VMEM] * 4 + [HBM] * len(out),
                out_specs=HBM,
                input_output_aliases={4: 0} if out else {},
                scratch_shapes=[
                    pltpu.VMEM((tokens, parts[c]), BF16),
                    pltpu.SemaphoreType.DMA((tokens // (2 * GROUP),)),
                ],
            )
        ]
    return out[0]


def solution(mesh):
    placed = (
        P(("ctx", "head"), None),
        P(("ctx", "head"), None),
        P("ctx", "head"),
        P(None, "ctx"),
        P(None, "head"),
    )
    return jax.shard_map(
        layer, mesh=mesh, in_specs=placed, out_specs=P("ctx", "head"), check_vma=False
    )
```
